32 devices in a mesh: dp: 4 (over x, core), shard: 2 (over y), seq: 4 (over z).
Axes of the slice: x: 2, y: 2, z: 4, core: 2. Of those that a mesh axis runs over, the one named last changes fastest.
Arguments:
- image_tokens: bfloat16 [16, 580, 1024], P(('dp', 'shard'), 'seq'), may hold values from -6 to 6
- cotangent: bfloat16 [16, 580, 1024], P(('dp', 'shard'), 'seq'), may hold values from -6 to 6
- ln1_gain: bfloat16 [2, 1024], P(None, ('shard', 'seq')), may hold values from 0.25 to 1.75
- ln1_bias: bfloat16 [2, 1024], P(None, ('shard', 'seq')), may hold values from -1.5 to 1.5
- qkv_weight: bfloat16 [2, 1024, 3072], P(None, ('shard', 'seq')), may hold values from -0.1875 to 0.1875
- qv_bias: bfloat16 [2, 2, 1024], P(None, None, ('shard', 'seq')), may hold values from -1.5 to 1.5
- proj_weight: bfloat16 [2, 1024, 1024], P(None, ('shard', 'seq')), may hold values from -1.5 to 1.5
- proj_bias: bfloat16 [2, 1024], P(None, ('shard', 'seq')), may hold values from -1.5 to 1.5
- ln2_gain: bfloat16 [2, 1024], P(None, ('shard', 'seq')), may hold values from 0.25 to 1.75
- ln2_bias: bfloat16 [2, 1024], P(None, ('shard', 'seq')), may hold values from -1.5 to 1.5
- fc1_weight: bfloat16 [2, 1024, 4096], P(None, ('shard', 'seq')), may hold values from -0.1875 to 0.1875
- fc1_bias: bfloat16 [2, 4096], P(None, ('shard', 'seq')), may hold values from -2.5 to 2.5
- fc2_weight: bfloat16 [2, 4096, 1024], P(None, ('shard', 'seq')), may hold values from -0.09375 to 0.09375
- fc2_bias: bfloat16 [2, 1024], P(None, ('shard', 'seq')), may hold values from -1.5 to 1.5
Outputs:
- output: float32 [16, 580, 1024], P(('dp', 'shard'), 'seq')
- input_grad: float32 [16, 580, 1024], P(('dp', 'shard'), 'seq')
- grad_ln1_gain: float32 [2, 1024], P(None, ('shard', 'seq'))
- grad_ln1_bias: float32 [2, 1024], P(None, ('shard', 'seq'))
- grad_qkv_weight: float32 [2, 1024, 3072], P(None, ('shard', 'seq'))
- grad_qv_bias: float32 [2, 2, 1024], P(None, None, ('shard', 'seq'))
- grad_proj_weight: float32 [2, 1024, 1024], P(None, ('shard', 'seq'))
- grad_proj_bias: float32 [2, 1024], P(None, ('shard', 'seq'))
- grad_ln2_gain: float32 [2, 1024], P(None, ('shard', 'seq'))
- grad_ln2_bias: float32 [2, 1024], P(None, ('shard', 'seq'))
- grad_fc1_weight: float32 [2, 1024, 4096], P(None, ('shard', 'seq'))
- grad_fc1_bias: float32 [2, 4096], P(None, ('shard', 'seq'))
- grad_fc2_weight: float32 [2, 4096, 1024], P(None, ('shard', 'seq'))
- grad_fc2_bias: float32 [2, 1024], P(None, ('shard', 'seq'))
The draws below stay inside these ranges and needn't reach their ends.
All inputs are finite; a program needn't handle non-finite values.
Results may differ from the reference program's by a relative error of at most 0.015.
Values may be sent and summed in bfloat16 or wider, within the bound.
No kernel may reach another device: no remote copies, remote signals or barrier semaphores. Data moves between devices by JAX's collectives and lax.ppermute only.
A program may use at most 256 MiB of HBM per device.

```python
import jax
import jax.numpy as jnp
from jax import lax

D = 1024
FF = 4096
HEADS = 16
HEAD_DIM = 64
SEQ = 577
LAYERS = 2
SEQ_PAD = 580
IMAGES = 16


def shard_levels(rng, extent, shards, smallest, high):
    def one(position, blocks):
        draws = jax.random.uniform(jax.random.fold_in(jax.random.fold_in(rng, 6), position), (blocks,), jnp.float32, smallest / len(shards), high / len(shards))
        return jnp.repeat(jnp.exp(draws), extent[position] // blocks).reshape((-1,) + (1,) * (len(extent) - position - 1))

    factor_of = one(*shards[0])
    for cut in shards[1:]:
        factor_of = factor_of * one(*cut)
    return factor_of


def gaussian(rng, shape, deviation, reach, split=(), kind=jnp.bfloat16):
    entries = jax.random.normal(rng, shape, jnp.float32) * deviation
    if len(split) > 0:
        entries = shard_levels(rng, shape, split, -0.22, 0.18) * entries
    return jnp.clip(entries, min=-reach, max=reach).astype(kind)


def setup_inputs(seed: int = 0) -> dict:
    keys = jax.random.split(jax.random.key(seed), 15)
    image_tokens = gaussian(keys[0], (IMAGES, SEQ_PAD, D), 1.0, 6.0, ((0, 8), (1, 4)))
    cotangent = gaussian(keys[1], (IMAGES, SEQ_PAD, D), 1.0, 6.0, ((0, 8), (1, 4)))
    ln1_gain = jnp.clip(1.0 + 0.15 * jax.random.normal(keys[2], (LAYERS, D), jnp.float32), 0.25, 1.75).astype(jnp.bfloat16)
    ln1_bias = gaussian(keys[3], (LAYERS, D), 0.3, 1.5, ((1, 8),))
    qkv_weight = gaussian(keys[4], (LAYERS, D, 3 * D), D ** -0.5, 0.1875, ((1, 8),))
    qv_bias = gaussian(keys[5], (LAYERS, 2, D), 0.3, 1.5, ((2, 8),))
    proj_weight = gaussian(keys[6], (LAYERS, D, D), (max(D // 64, 4)) ** -0.5, 1.5, ((1, 8),))
    proj_bias = gaussian(keys[7], (LAYERS, D), 0.3, 1.5, ((1, 8),))
    ln2_gain = jnp.clip(1.0 + 0.15 * jax.random.normal(keys[8], (LAYERS, D), jnp.float32), 0.25, 1.75).astype(jnp.bfloat16)
    ln2_bias = gaussian(keys[9], (LAYERS, D), 0.3, 1.5, ((1, 8),))
    fc1_weight = gaussian(keys[10], (LAYERS, D, FF), D ** -0.5, 0.1875, ((1, 8),))
    fc1_bias = gaussian(keys[11], (LAYERS, FF), 0.5, 2.5, ((1, 8),))
    fc2_weight = gaussian(keys[12], (LAYERS, FF, D), FF ** -0.5, 0.09375, ((1, 8),))
    fc2_bias = gaussian(keys[13], (LAYERS, D), 0.3, 1.5, ((1, 8),))
    return {"image_tokens": image_tokens, "cotangent": cotangent, "ln1_gain": ln1_gain, "ln1_bias": ln1_bias, "qkv_weight": qkv_weight, "qv_bias": qv_bias, "proj_weight": proj_weight, "proj_bias": proj_bias, "ln2_gain": ln2_gain, "ln2_bias": ln2_bias, "fc1_weight": fc1_weight, "fc1_bias": fc1_bias, "fc2_weight": fc2_weight, "fc2_bias": fc2_bias}


epsilon = 1e-06
masked_score = -1e+30

@jax.custom_vjp
def low(v):
    return lax.optimization_barrier(v.astype(jnp.bfloat16)).astype(jnp.float32)

@jax.custom_vjp
def low_back(v):
    return v

def low_keep(v):
    return (low(v), None)

def low_pass(kept, grad):
    return (grad,)

def back_keep(v):
    return (v, None)

def back_low(kept, grad):
    return (low(grad),)
low.defvjp(low_keep, low_pass)
low_back.defvjp(back_keep, back_low)

def exact_dot(left, right):
    return jnp.matmul(left, right, precision=lax.Precision.HIGHEST)

def norm_rows(stream, gain, offset):
    center = stream - lax.optimization_barrier(jnp.mean(stream, axis=-1, keepdims=True))
    spread = lax.optimization_barrier(jnp.mean(center * center, axis=-1, keepdims=True))
    return center * lax.rsqrt(spread + epsilon) * gain + offset

def rounded(value):
    return low_back(low(value))

def block(stream, params, key_live):
    gain_one, bias_one, qkv_mat, qv_add, proj_mat, proj_add, gain_two, bias_two, hidden_mat, hidden_add, output_mat, output_add = params
    score_scale = HEAD_DIM ** (-0.5)
    first_in = low(norm_rows(stream, gain_one, bias_one))
    projected = exact_dot(first_in, qkv_mat)
    queries = rounded((projected[:, :D] + qv_add[0]) * score_scale)
    own_keys = rounded(projected[:, D:2 * D])
    own_values = rounded(projected[:, 2 * D:] + qv_add[1])
    query_heads = queries.reshape(-1, HEADS, HEAD_DIM)
    key_heads = own_keys.reshape(-1, HEADS, HEAD_DIM)
    value_heads = own_values.reshape(-1, HEADS, HEAD_DIM)
    scores = low_back(jnp.einsum('qhd,khd->hqk', query_heads, key_heads, precision=lax.Precision.HIGHEST))
    scores = jnp.where(key_live, scores, masked_score)
    attn_probs = low(jax.nn.softmax(scores, axis=-1))
    head_mixed = jnp.einsum('hqk,khd->qhd', attn_probs, value_heads, precision=lax.Precision.HIGHEST)
    attn_out = rounded(head_mixed.reshape(stream.shape))
    middle = stream + low_back(exact_dot(attn_out, proj_mat) + proj_add)
    second_in = low(norm_rows(middle, gain_two, bias_two))
    pre_act = low_back(exact_dot(second_in, hidden_mat) + hidden_add)
    hidden = low(jax.nn.gelu(pre_act, approximate=False))
    return middle + low_back(exact_dot(hidden, output_mat) + output_add)

def reference(image_tokens, cotangent, ln1_gain, ln1_bias, qkv_weight, qv_bias, proj_weight, proj_bias, ln2_gain, ln2_bias, fc1_weight, fc1_bias, fc2_weight, fc2_bias):
    params = tuple((member.astype(jnp.float32) for member in (ln1_gain, ln1_bias, qkv_weight, qv_bias, proj_weight, proj_bias, ln2_gain, ln2_bias, fc1_weight, fc1_bias, fc2_weight, fc2_bias)))
    key_live = jnp.arange(SEQ_PAD) < SEQ
    row_live = key_live.astype(jnp.float32)[:, None]

    def forward(stream, weights):
        for layer_at in range(LAYERS):
            stream = block(stream, tuple((member[layer_at] for member in weights)), key_live)
        return stream

    def one_image(totals, image_pair):
        tokens, seed_grad = image_pair
        result, pull_back = jax.vjp(forward, tokens.astype(jnp.float32), params)
        stream_grad, weight_grads = pull_back(seed_grad.astype(jnp.float32) * row_live)
        totals = tuple((total_part + new_part for total_part, new_part in zip(totals, weight_grads)))
        return (totals, (result, stream_grad))
    zero_grads = tuple((jnp.zeros_like(member) for member in params))
    totals, (outputs, input_grads) = lax.scan(one_image, zero_grads, (image_tokens, cotangent))
    return (outputs, input_grads) + totals
```

```python
import functools

import jax
import jax.numpy as jnp
from jax import lax
from jax.experimental import pallas as pl
from jax.experimental.pallas import tpu as pltpu
from jax.sharding import Mesh, PartitionSpec as P

HEAD_DIM = 64
SEQ = 577
CORES = 2

epsilon = 1e-06
masked_score = -1e30


BF = jnp.bfloat16
F32 = jnp.float32


def shifted(values, axis, step):
    size = lax.axis_size(axis)
    return lax.ppermute(values, axis, [(at, (at + step) % size) for at in range(size)])


def swap_cores(values):
    return lax.ppermute(values, "core", [(0, 1), (1, 0)])


def place(parts, axis):
    size = len(parts)
    if size == 1:
        return parts[0][None]
    at = lax.axis_index(axis)
    if size == 2:
        return jnp.stack(
            [
                jnp.where(at == 0, parts[0], parts[1]),
                jnp.where(at == 0, parts[1], parts[0]),
            ]
        )
    whole = jnp.zeros((size,) + parts[0].shape, parts[0].dtype)
    for step, part in enumerate(parts):
        whole = lax.dynamic_update_index_in_dim(whole, part, (at - step) % size, 0)
    return whole


def spread(own, axis):
    size = lax.axis_size(axis)
    return place([own] + [shifted(own, axis, step) for step in range(1, size)], axis)


def shared_width(columns, numerator, denominator):
    reps = lax.axis_size("rep")
    if reps == 1:
        return 0
    return columns * numerator // (denominator * reps) // 128 * 128


def gather_rows(own):
    rows, columns = own.shape
    reps = lax.axis_size("rep")
    width = shared_width(columns, 3, 4)
    alone = columns - reps * width
    if width:
        part = lax.dynamic_slice_in_dim(own, alone + lax.axis_index("rep") * width, width, 1)
        own = jnp.concatenate([own[:, :alone], part], axis=1)
    plane = spread(own, "seq")
    both = spread(plane, "shard").reshape(-1, alone + width)
    if not width:
        return both
    parts = spread(both[:, alone:], "rep")
    return jnp.concatenate([both[:, :alone]] + [parts[at] for at in range(reps)], axis=1)


def gather_small(own):
    plane = spread(own, "seq")
    both = spread(plane, "shard")
    return both.reshape((-1,) + own.shape)


def block_of(values, axis, step):
    size = lax.axis_size(axis)
    rows = values.shape[0] // size
    at = (lax.axis_index(axis) + step) % size
    return lax.dynamic_slice_in_dim(values, at * rows, rows, 0)


def owner_total(values, axis, out_type):
    size = lax.axis_size(axis)
    total = block_of(values, axis, 0).astype(F32)
    for step in range(1, size):
        total = total + shifted(block_of(values, axis, step), axis, step).astype(F32)
    return total.astype(out_type)


def reduce_rows(terms):
    columns = terms.shape[1]
    reps = lax.axis_size("rep")
    width = shared_width(columns, 1, 2)
    alone = columns - reps * width
    rep = lax.axis_index("rep")
    if width:

        def part_of(step):
            at = (rep + step) % reps
            return lax.dynamic_slice_in_dim(terms, alone + at * width, width, 1)

        total = part_of(0).astype(F32)
        for step in range(1, reps):
            total = total + shifted(part_of(step), "rep", step).astype(F32)
        terms = jnp.concatenate([terms[:, :alone], total.astype(BF)], axis=1)
    own = owner_total(owner_total(terms, "shard", BF), "seq", BF)
    every = spread(own, "rep")
    first = sum(every[at, :, :alone].astype(F32) for at in range(reps)).astype(BF)
    if not width:
        return first
    return jnp.concatenate([first] + [every[at, :, alone:] for at in range(reps)], axis=1)


def both_cores(own, axis):
    other = swap_cores(own)
    first = lax.axis_index("core") == 0
    halves = [jnp.where(first, own, other), jnp.where(first, other, own)]
    return jnp.stack(halves, axis=axis).astype(F32)


def normed(stream, gain, offset):
    center = stream - jnp.mean(stream, axis=-1, keepdims=True)
    spread_of = jnp.mean(center * center, axis=-1, keepdims=True)
    return center * lax.rsqrt(spread_of + epsilon) * gain + offset


def norm_back(stream, gain, grad):
    center = stream - jnp.mean(stream, axis=-1, keepdims=True)
    spread_of = jnp.mean(center * center, axis=-1, keepdims=True)
    inverse = lax.rsqrt(spread_of + epsilon)
    hat = center * inverse
    scaled = grad * gain
    back = inverse * (
        scaled
        - jnp.mean(scaled, axis=-1, keepdims=True)
        - hat * jnp.mean(scaled * hat, axis=-1, keepdims=True)
    )
    return back, jnp.sum(grad * hat, axis=0), jnp.sum(grad, axis=0)


def exact_gelu(values):
    return jax.nn.gelu(values, approximate=False)


def dot(left, right, left_at, right_at):
    return lax.dot_general(
        left, right, (((left_at,), (right_at,)), ((), ())), preferred_element_type=F32
    )


def softmax_of(query, key, dead):
    scores = dot(query, key, 1, 1)
    scores = jnp.where(dead, masked_score, scores)
    raised = jnp.exp(scores - jnp.max(scores, axis=1, keepdims=True))
    return raised / jnp.sum(raised, axis=1, keepdims=True)


def attend_kernel(live_ref, query_ref, key_ref, value_ref, out_ref):
    dead = live_ref[...] == 0.0
    outs = []
    for at in range(query_ref.shape[1] // HEAD_DIM):
        lanes = slice(at * HEAD_DIM, (at + 1) * HEAD_DIM)
        probs = softmax_of(query_ref[:, lanes], key_ref[:, lanes], dead).astype(BF)
        outs.append(dot(probs, value_ref[:, lanes], 1, 0))
    out_ref[...] = jnp.concatenate(outs, axis=1).astype(out_ref.dtype)


def attend_back_kernel(
    live_ref, query_ref, key_ref, value_ref, grad_ref, query_out, key_out, value_out
):
    dead = live_ref[...] == 0.0
    outs = ([], [], [])
    for at in range(query_ref.shape[1] // HEAD_DIM):
        lanes = slice(at * HEAD_DIM, (at + 1) * HEAD_DIM)
        query, key, value = query_ref[:, lanes], key_ref[:, lanes], value_ref[:, lanes]
        grad = grad_ref[:, lanes]
        probs = softmax_of(query, key, dead)
        prob_grad = dot(grad, value, 1, 1)
        inner = jnp.sum(probs * prob_grad, axis=1, keepdims=True)
        score_grad = (probs * (prob_grad - inner)).astype(BF)
        outs[0].append(dot(score_grad, key, 1, 0).astype(BF).astype(F32) * HEAD_DIM**-0.5)
        outs[1].append(dot(score_grad, query, 0, 0))
        outs[2].append(dot(probs.astype(BF), grad, 0, 0))
    for ref, parts in zip((query_out, key_out, value_out), outs):
        ref[...] = jnp.concatenate(parts, axis=1).astype(ref.dtype)


def attention(live, qkv):
    rows, columns = qkv.shape
    lanes = 2 * HEAD_DIM
    steps = columns // 3 // lanes

    def third(which):
        return pl.BlockSpec((rows, lanes), lambda at: (0, at + which * steps))

    return pl.pallas_call(
        attend_kernel,
        grid=(steps,),
        in_specs=[pl.BlockSpec((1, rows), lambda at: (0, 0)), third(0), third(1), third(2)],
        out_specs=third(0),
        out_shape=jax.ShapeDtypeStruct((rows, columns // 3), BF),
        cost_estimate=pl.CostEstimate(
            flops=4 * rows * rows * columns // 3,
            bytes_accessed=rows * columns * 3,
            transcendentals=rows * rows * columns // 3 // HEAD_DIM,
        ),
        name="attend",
    )(live, qkv, qkv, qkv)


def attention_back(live, qkv, grad):
    rows, columns = qkv.shape
    lanes = 2 * HEAD_DIM
    steps = columns // 3 // lanes

    def third(which):
        return pl.BlockSpec((rows, lanes), lambda at: (0, at + which * steps))

    out = jax.ShapeDtypeStruct((rows, columns // 3), BF)
    return pl.pallas_call(
        attend_back_kernel,
        grid=(steps,),
        in_specs=[
            pl.BlockSpec((1, rows), lambda at: (0, 0)),
            third(0),
            third(1),
            third(2),
            third(0),
        ],
        out_specs=[third(0)] * 3,
        out_shape=[out] * 3,
        cost_estimate=pl.CostEstimate(
            flops=10 * rows * rows * columns // 3,
            bytes_accessed=rows * columns * 5,
            transcendentals=rows * rows * columns // 3 // HEAD_DIM,
        ),
        name="attend_back",
    )(live, qkv, qkv, qkv, grad)


def row_sum(values):
    return jnp.sum(values.astype(F32), axis=0)


def pair_rows(own):
    return jnp.concatenate([own, swap_cores(own)], axis=0)


def pair_total(terms):
    rows = terms.shape[0] // CORES
    return terms[:rows] + swap_cores(terms[rows:].astype(BF)).astype(F32)


def column_trips(images):
    size = lax.axis_size("seq")
    trips = []
    for turn in range(images):
        pairs = []
        for core in range(CORES):
            for seq in range(size):
                image = (turn + seq) % images
                to_core, to_seq = seq // images, core * images + image
                pairs.append((core * size + seq, to_core * size + to_seq))
        trips.append(pairs)
    return trips


def to_chip(values, trips):
    images = values.shape[0]
    seq = lax.axis_index("seq")
    parts = []
    for turn, pairs in enumerate(trips):
        part = lax.dynamic_index_in_dim(values, (turn + seq) % images, 0, keepdims=False)
        parts.append(lax.ppermute(part, ("core", "seq"), pairs))
    return jnp.concatenate(parts, axis=0)


def from_chip(values, trips):
    images = len(trips)
    rows = values.shape[0] // images
    seq = lax.axis_index("seq")
    back = [
        lax.ppermute(
            values[turn * rows : (turn + 1) * rows],
            ("core", "seq"),
            [(there, here) for here, there in pairs],
        )
        for turn, pairs in enumerate(trips)
    ]
    stacked = jnp.stack(back)
    return jnp.stack(
        [
            lax.dynamic_index_in_dim(stacked, (image - seq) % images, 0, keepdims=False)
            for image in range(images)
        ]
    ).astype(F32)


def half(values, axis):
    return lax.dynamic_index_in_dim(values, lax.axis_index("core"), axis, keepdims=False)


def on_device(
    image_tokens,
    cotangent,
    ln1_gain,
    ln1_bias,
    qkv_weight,
    qv_bias,
    proj_weight,
    proj_bias,
    ln2_gain,
    ln2_bias,
    fc1_weight,
    fc1_bias,
    fc2_weight,
    fc2_bias,
):
    layers, own_width = ln1_gain.shape
    width = proj_weight.shape[2]
    hidden_width = fc1_weight.shape[2]
    shards = width // own_width
    images, rows_here = image_tokens.shape[:2]
    seq_size = lax.axis_size("seq")
    assert images * CORES == seq_size
    core, seq = lax.axis_index("core"), lax.axis_index("seq")
    trips = column_trips(images)

    small = jnp.concatenate(
        [
            member.reshape(layers, -1, own_width)
            for member in (
                ln1_gain,
                ln1_bias,
                qv_bias,
                proj_bias,
                ln2_gain,
                ln2_bias,
                fc2_bias,
                fc1_bias,
            )
        ],
        axis=1,
    )
    small = gather_small(small)

    def vector(layer, at):
        return small[:, layer, at].reshape(-1).astype(F32)

    def half_vector(layer, at):
        return half(small[:, layer, at].reshape(shards, CORES, -1), 1).reshape(-1).astype(F32)

    def small_of(layer):
        return (
            vector(layer, 0),
            vector(layer, 1),
            half_vector(layer, 2),
            half_vector(layer, 3),
            vector(layer, 4),
            vector(layer, 5),
            vector(layer, 6),
            vector(layer, 7),
            half(small[:, layer, 8:].reshape(shards, CORES, -1), 1).reshape(-1).astype(F32),
        )

    def weights_of(layer):
        qkv = half(qkv_weight[layer].reshape(own_width, 3, -1, CORES, HEAD_DIM), 3)
        proj = half(proj_weight[layer].reshape(CORES, -1, width), 0)
        fc1 = half(
            fc1_weight[layer].reshape(own_width, shards, CORES, hidden_width // shards // CORES),
            2,
        )
        fc2 = half(fc2_weight[layer].reshape(CORES, -1, width), 0)
        return (
            gather_rows(qkv.reshape(own_width, -1)),
            gather_rows(proj),
            gather_rows(fc1.reshape(own_width, -1)),
            gather_rows(fc2),
        )

    stream = to_chip(image_tokens, trips).astype(F32)
    grad_stream = to_chip(cotangent, trips).astype(F32)

    def positions(which):
        turns = [
            (which * images + (seq - turn) % images) * rows_here + jnp.arange(rows_here)
            for turn in range(images)
        ]
        return jnp.concatenate(turns)

    own_live = (positions(core) < SEQ).astype(F32)
    other_live = (positions(1 - core) < SEQ).astype(F32)
    live = jnp.concatenate([own_live, other_live])[None]
    grad_stream = grad_stream * own_live[:, None]

    score_scale = HEAD_DIM**-0.5
    kept = []
    for layer in range(layers):
        gain_one, bias_one, q_add, v_add, proj_add, gain_two, bias_two, out_add, hid_add = (
            small_of(layer)
        )
        qkv_mat, proj_mat, hid_mat, out_mat = weights_of(layer)
        first_in = pair_rows(normed(stream, gain_one, bias_one).astype(BF))
        projected = dot(first_in, qkv_mat, 1, 0)
        part = q_add.shape[0]
        qkv = jnp.concatenate(
            [
                (projected[:, :part] + q_add) * score_scale,
                projected[:, part : 2 * part],
                projected[:, 2 * part :] + v_add,
            ],
            axis=1,
        ).astype(BF)
        attn_out = attention(live, qkv)
        middle = stream + pair_total(dot(attn_out, proj_mat, 1, 0)) + proj_add
        second_in = pair_rows(normed(middle, gain_two, bias_two).astype(BF))
        pre_act = dot(second_in, hid_mat, 1, 0) + hid_add
        hidden = exact_gelu(pre_act).astype(BF)
        result = middle + pair_total(dot(hidden, out_mat, 1, 0)) + out_add
        kept.append(
            (
                (stream, first_in, qkv, attn_out, middle, second_in, pre_act, hidden),
                (gain_one, gain_two),
                (qkv_mat, proj_mat, hid_mat, out_mat),
            )
        )
        stream = result
    output = from_chip(stream.astype(BF), trips)

    large = [None] * layers
    small_terms = [None] * layers
    for layer in reversed(range(layers)):
        saved, gains, mats = kept[layer]
        stream, first_in, qkv, attn_out, middle, second_in, pre_act, hidden = saved
        gain_one, gain_two = gains
        qkv_mat, proj_mat, hid_mat, out_mat = mats
        branch_own = grad_stream.astype(BF)
        branch = pair_rows(branch_own)
        out_grad = dot(hidden, branch, 0, 0).astype(BF)
        out_owned = reduce_rows(out_grad)
        hidden_grad = dot(branch, out_mat, 1, 1)
        pre_grad = jax.vjp(exact_gelu, pre_act)[1](hidden_grad)[0].astype(BF)
        hid_grad = dot(second_in, pre_grad, 0, 0).astype(BF)
        hid_owned = reduce_rows(hid_grad)
        second_grad = pair_total(dot(pre_grad, hid_mat, 1, 1))
        back, grad_gain_two, grad_bias_two = norm_back(middle, gain_two, second_grad)
        middle_grad = grad_stream + back
        proj_own = middle_grad.astype(BF)
        proj_grad = pair_rows(proj_own)
        proj_owned = reduce_rows(dot(attn_out, proj_grad, 0, 0).astype(BF))
        attn_grad = dot(proj_grad, proj_mat, 1, 1).astype(BF)
        query_grad, key_grad, value_grad = attention_back(live, qkv, attn_grad)
        qkv_grad = jnp.concatenate([query_grad, key_grad, value_grad], axis=1)
        qkv_owned = reduce_rows(dot(first_in, qkv_grad, 0, 0).astype(BF))
        first_grad = pair_total(dot(qkv_grad, qkv_mat, 1, 1))
        back, grad_gain_one, grad_bias_one = norm_back(stream, gain_one, first_grad)

        def by_core(vector_half):
            mine = vector_half.reshape(shards, -1)
            none = jnp.zeros_like(mine)
            pair = [jnp.where(core == at, mine, none) for at in range(CORES)]
            return jnp.stack(pair, axis=1).reshape(shards, -1, own_width)

        def by_owner(vector_whole):
            return vector_whole.reshape(shards, 1, own_width)

        small_terms[layer] = jnp.concatenate(
            [
                by_owner(grad_gain_one),
                by_owner(grad_bias_one),
                by_core(row_sum(query_grad)),
                by_core(row_sum(value_grad)),
                by_owner(row_sum(proj_own)),
                by_owner(grad_gain_two),
                by_owner(grad_bias_two),
                by_owner(row_sum(branch_own)),
                by_core(row_sum(pre_grad)),
            ],
            axis=1,
        )
        large[layer] = (qkv_owned, proj_owned, hid_owned, out_owned)
        grad_stream = middle_grad + back
    input_grad = from_chip(grad_stream.astype(BF), trips)

    def merged(at, shape, axis, final):
        own = jnp.stack([large[layer][at] for layer in range(layers)])
        return both_cores(own.reshape((layers,) + shape), axis).reshape((layers,) + final)

    grad_qkv = merged(0, (own_width, 3, -1, HEAD_DIM), 4, (own_width, -1))
    grad_proj = merged(1, (-1, width), 1, (-1, width))
    grad_fc1 = merged(2, (own_width, shards, hidden_width // shards // CORES), 3, (own_width, -1))
    grad_fc2 = merged(3, (-1, width), 1, (-1, width))

    terms = jnp.stack(small_terms, axis=1)
    terms = terms + swap_cores(terms)
    terms = jnp.sum(spread(terms, "rep"), axis=0)
    owned = owner_total(owner_total(terms, "shard", F32), "seq", F32)[0]

    def member(at, count=1):
        return owned[:, at : at + count].reshape(layers, -1)

    return (
        output,
        input_grad,
        member(0),
        member(1),
        grad_qkv,
        owned[:, 2:4],
        grad_proj,
        member(4),
        member(5),
        member(6),
        grad_fc1,
        member(8, fc1_bias.shape[1] // own_width),
        grad_fc2,
        member(7),
    )


def solution(mesh):
    dp, shard, seq = (mesh.shape[name] for name in ("dp", "shard", "seq"))
    cores = Mesh(
        mesh.devices.reshape(dp // CORES, CORES, shard, seq), ("rep", "core", "shard", "seq")
    )
    images = P(("rep", "core", "shard"), "seq", None)
    vectors = P(None, ("shard", "seq"))
    matrices = P(None, ("shard", "seq"), None)
    pairs = P(None, None, ("shard", "seq"))
    params = (
        vectors,
        vectors,
        matrices,
        pairs,
        matrices,
        vectors,
        vectors,
        vectors,
        matrices,
        vectors,
        matrices,
        vectors,
    )
    return jax.shard_map(
        on_device,
        mesh=cores,
        in_specs=(images, images) + params,
        out_specs=(images, images) + params,
        check_vma=False,
    )
```

```python
import functools

import jax
import jax.numpy as jnp
from jax import lax
from jax.experimental import pallas as pl
from jax.experimental.pallas import tpu as pltpu
from jax.sharding import Mesh, PartitionSpec as P

HEAD_DIM = 64
SEQ = 577
CORES = 2

epsilon = 1e-06
masked_score = -1e30


BF = jnp.bfloat16
F32 = jnp.float32


def flip_pairs(axis, bit):
    return [(at, at ^ bit) for at in range(lax.axis_size(axis))]


def flipped(values, axis, bit):
    return lax.ppermute(values, axis, flip_pairs(axis, bit))


def swap_cores(values):
    return flipped(values, "core", 1)


def bits_of(axis):
    size = lax.axis_size(axis)
    assert size & (size - 1) == 0
    return [1 << at for at in reversed(range(size.bit_length() - 1))]


def is_low(axis, bit):
    return (lax.axis_index(axis) & bit) == 0


def ordered(own, other, axis, bit, at):
    low = is_low(axis, bit)
    return jnp.stack([jnp.where(low, own, other), jnp.where(low, other, own)], axis=at)


class Task:
    def __init__(self, steps):
        self.steps, self.value, self.done = steps, None, False
        self.send, self.there = None, None
        self.advance()

    def advance(self):
        try:
            self.send = self.steps.send(self.there)
        except StopIteration as stop:
            self.value, self.done, self.send = stop.value, True, None


class Line:
    def __init__(self):
        self.tasks = []

    def add(self, steps):
        task = Task(steps)
        self.tasks.append(task)
        return task

    def tick(self, *fresh):
        for task in self.tasks:
            if task.there is not None:
                task.advance()
        self.tasks = [task for task in self.tasks if not task.done]
        sends = [task.send[2] for task in self.tasks]
        sends, fresh = lax.optimization_barrier((sends, fresh))
        for task, values in zip(self.tasks, sends):
            task.there = lax.ppermute(values, task.send[0], task.send[1])
        return fresh


def shared_width(columns, numerator, denominator):
    if lax.axis_size("rep") != 2:
        return 0
    return columns * numerator // (denominator * 2) // 128 * 128


def rep_part(values, alone, width, own):
    low = is_low("rep", 1)
    parts = values[..., alone : alone + width], values[..., alone + width :]
    return jnp.where(low, *(parts if own else parts[::-1]))


def places():
    return jnp.stack([lax.axis_index(axis) for axis in ("shard", "seq", "rep")]).astype(jnp.int32)


def rank_in_plane(step, size):
    rank, bit = 0, 1
    while bit < size:
        rank = rank * 2 + (step // bit) % 2
        bit *= 2
    return rank


def copy_kernel_params(limit=None):
    return pltpu.CompilerParams(vmem_limit_bytes=limit)


def finish_gather(near, far, cross, alone, width):
    seqs = lax.axis_size("seq")
    rows = near.shape[0] // seqs
    held = near.shape[1]
    columns = alone + 2 * width if width else held

    def kernel(place, near_ref, far_ref, *refs):
        cross_ref, out_ref = (refs[0], refs[1]) if width else (None, refs[0])
        away = (pl.program_id(0) // seqs) ^ place[0]

        def fill(source):
            if not width:
                out_ref[...] = source[...]
                return
            out_ref[:, :alone] = source[:, :alone]

            @pl.when(place[2] == 0)
            def _():
                out_ref[:, alone : alone + width] = source[:, alone:]
                out_ref[:, alone + width :] = cross_ref[...]

            @pl.when(place[2] == 1)
            def _():
                out_ref[:, alone : alone + width] = cross_ref[...]
                out_ref[:, alone + width :] = source[:, alone:]

        pl.when(away == 0)(lambda: fill(near_ref))
        pl.when(away == 1)(lambda: fill(far_ref))

    def rank(at, place):
        return rank_in_plane((at % seqs) ^ place[1], seqs)

    plane = pl.BlockSpec((rows, held), lambda at, place: (rank(at, place), 0))
    specs, given = [plane, plane], [near, far]
    if width:
        specs.append(
            pl.BlockSpec(
                (rows, width),
                lambda at, place: (((at // seqs) ^ place[0]) * seqs + rank(at, place), 0),
            )
        )
        given.append(cross)
    return pl.pallas_call(
        kernel,
        grid_spec=pltpu.PrefetchScalarGridSpec(
            num_scalar_prefetch=1,
            grid=(2 * seqs,),
            in_specs=specs,
            out_specs=pl.BlockSpec((rows, columns), lambda at, place: (at, 0)),
        ),
        out_shape=jax.ShapeDtypeStruct((2 * seqs * rows, columns), BF),
        cost_estimate=pl.CostEstimate(
            flops=0, transcendentals=0, bytes_accessed=2 * seqs * rows * (columns + held + width) * 2
        ),
        name="finish_gather",
    )(places(), *given)


def gather_steps(own):
    columns = own.shape[1]
    width = shared_width(columns, 2, 3)
    alone = columns - 2 * width
    plane = own
    if width:
        plane = jnp.concatenate([own[:, :alone], rep_part(own, alone, width, True)], axis=1)
    for bit in bits_of("seq"):
        there = yield "seq", flip_pairs("seq", bit), plane
        plane = jnp.concatenate([plane, there], axis=0)
    far = yield "shard", flip_pairs("shard", 1), plane
    cross = None
    if width:
        cross = jnp.concatenate([plane[:, alone:], far[:, alone:]], axis=0)
        cross = yield "rep", flip_pairs("rep", 1), cross
    return finish_gather(plane, far, cross, alone, width)


def folded(ref, cross_ref, place, alone, width):
    if not width:
        return [(slice(None), None, lambda: ref[...].astype(F32))]
    there = lambda: cross_ref[...].astype(F32)
    return [
        (slice(0, alone), None, lambda: ref[:, :alone].astype(F32)),
        (
            slice(alone, None),
            place[2] == 0,
            lambda: ref[:, alone : alone + width].astype(F32) + there(),
        ),
        (slice(alone, None), place[2] == 1, lambda: ref[:, alone + width :].astype(F32) + there()),
    ]


def guarded(condition, body):
    if condition is None:
        body()
    else:
        pl.when(condition)(body)


def fold_for_far(terms, cross, alone, width):
    seqs = lax.axis_size("seq")
    rows, columns = terms.shape[0] // (2 * seqs), terms.shape[1]

    def kernel(place, ref, *refs):
        cross_ref, out_ref = (refs[0], refs[1]) if width else (None, refs[0])
        for lanes, condition, value in folded(ref, cross_ref, place, alone, width):

            def store(lanes=lanes, value=value):
                out_ref[:, lanes] = value().astype(BF)

            guarded(condition, store)

    at_far = lambda at, place: ((1 - place[0]) * seqs + at, 0)
    specs, given = [pl.BlockSpec((rows, columns), at_far)], [terms]
    if width:
        specs.append(pl.BlockSpec((rows, width), at_far))
        given.append(cross)
    return pl.pallas_call(
        kernel,
        grid_spec=pltpu.PrefetchScalarGridSpec(
            num_scalar_prefetch=1,
            grid=(seqs,),
            in_specs=specs,
            out_specs=pl.BlockSpec((rows, alone + width), lambda at, place: (at, 0)),
        ),
        out_shape=jax.ShapeDtypeStruct((seqs * rows, alone + width), BF),
        cost_estimate=pl.CostEstimate(
            flops=0, transcendentals=0, bytes_accessed=seqs * rows * columns * 5
        ),
        name="fold_for_far",
    )(places(), *given)


def fold_own(terms, cross, far, alone, width):
    seqs = lax.axis_size("seq")
    rows, columns = terms.shape[0] // (2 * seqs), terms.shape[1]
    held = alone + width

    def kernel(place, *refs):
        outs = refs[-2:]
        per = 3 if width else 2
        for side, out_ref in enumerate(outs):
            ref, far_ref = refs[side * per], refs[side * per + 1]
            cross_ref = refs[side * per + 2] if width else None
            for lanes, condition, value in folded(ref, cross_ref, place, alone, width):

                def store(lanes=lanes, value=value, out_ref=out_ref, far_ref=far_ref):
                    total = value() + far_ref[:, lanes].astype(F32)
                    out_ref[:, lanes] = total.astype(out_ref.dtype)

                guarded(condition, store)

    specs, given = [], []
    for side in range(2):
        near = lambda at, place, side=side: 2 * at + (place[1] + 1 - side) % 2
        whole = lambda at, place, near=near: (place[0] * seqs + near(at, place), 0)
        specs.append(pl.BlockSpec((rows, columns), whole))
        specs.append(pl.BlockSpec((rows, held), lambda at, place, near=near: (near(at, place), 0)))
        given += [terms, far]
        if width:
            specs.append(pl.BlockSpec((rows, width), whole))
            given.append(cross)
    out = pl.BlockSpec((rows, held), lambda at, place: (at, 0))
    shape = (seqs // 2 * rows, held)
    return pl.pallas_call(
        kernel,
        grid_spec=pltpu.PrefetchScalarGridSpec(
            num_scalar_prefetch=1, grid=(seqs // 2,), in_specs=specs, out_specs=[out, out]
        ),
        out_shape=[jax.ShapeDtypeStruct(shape, BF), jax.ShapeDtypeStruct(shape, F32)],
        cost_estimate=pl.CostEstimate(
            flops=0, transcendentals=0, bytes_accessed=seqs * rows * columns * 7
        ),
        name="fold_own",
    )(places(), *given)


def half_of(values, axis, bit, own):
    at = (lax.axis_index(axis) // bit) % 2
    return lax.dynamic_index_in_dim(values, at if own else 1 - at, 0, keepdims=False)


def owner_steps(values, axis, bits, out_type):
    for bit in bits:
        split = values.reshape((-1, 2) + values.shape[1:])
        split = jnp.moveaxis(split, 1, 0)
        send = half_of(split, axis, bit, False).astype(out_type)
        there = yield axis, flip_pairs(axis, bit), send
        values = half_of(split, axis, bit, True).astype(F32) + there.astype(F32)
    return values[0]


def spread_steps(own, axis):
    whole, lead = own, 0
    for bit in bits_of(axis):
        there = yield axis, flip_pairs(axis, bit), whole
        whole = ordered(whole, there, axis, bit, lead)
        lead += 1
    return whole.reshape((-1,) + own.shape)


def reduce_steps(terms):
    columns = terms.shape[1]
    seqs = lax.axis_size("seq")
    width = shared_width(columns, 1, 2)
    alone = columns - 2 * width
    cross = None
    if width:
        cross = rep_part(terms, alone, width, False)
        cross = yield "rep", flip_pairs("rep", 1), cross
    far = yield "shard", flip_pairs("shard", 1), fold_for_far(terms, cross, alone, width)
    send, keep = fold_own(terms, cross, far, alone, width)
    there = yield "seq", flip_pairs("seq", 1), send
    kept = (keep + there.astype(F32)).reshape(seqs // 2, -1, alone + width)
    bits = [bit // 2 for bit in reversed(bits_of("seq")) if bit > 1]
    for bit in bits:
        split = kept.reshape((-1, 2) + kept.shape[1:])
        at = (lax.axis_index("seq") // (2 * bit)) % 2
        send = lax.dynamic_index_in_dim(split, 1 - at, 1, keepdims=False).astype(BF)
        there = yield "seq", flip_pairs("seq", 2 * bit), send
        kept = lax.dynamic_index_in_dim(split, at, 1, keepdims=False) + there.astype(F32)
    own = kept[0].astype(BF)
    if width:
        there = yield "rep", flip_pairs("rep", 1), own
        first = (own[:, :alone].astype(F32) + there[:, :alone].astype(F32)).astype(BF)
        parts = ordered(own[:, alone:], there[:, alone:], "rep", 1, 0)
        own = jnp.concatenate([first, parts[0], parts[1]], axis=1)
    else:
        every = yield from spread_steps(own, "rep")
        own = jnp.sum(every.astype(F32), axis=0).astype(BF)
    other = yield "core", flip_pairs("core", 1), own
    return own, other


def small_steps(terms):
    there = yield "core", flip_pairs("core", 1), terms
    terms = terms + there
    every = yield from spread_steps(terms, "rep")
    terms = jnp.sum(every, axis=0)
    terms = yield from owner_steps(terms, "shard", reversed(bits_of("shard")), F32)
    return (yield from owner_steps(terms, "seq", reversed(bits_of("seq")), F32))


def spread(own, axis):
    whole, lead = own, 0
    for bit in bits_of(axis):
        whole = ordered(whole, flipped(whole, axis, bit), axis, bit, lead)
        lead += 1
    return whole.reshape((-1,) + own.shape)


def gather_small(own):
    return spread(spread(own, "seq"), "shard").reshape((-1,) + own.shape)


def merged_call(kernel, pieces, shapes, layers, layer, earlier, name):
    core = lax.axis_index("core").astype(jnp.int32)[None]
    given = list(pieces) + list(earlier)
    outs = [jax.ShapeDtypeStruct((layers,) + shape, F32) for shape in shapes]
    whole = lambda values: pl.BlockSpec(values.shape, lambda at, core: (0,) * values.ndim)

    def body(core_ref, *refs):
        kernel(core_ref[0], refs[: len(pieces)], [ref.at[0] for ref in refs[-len(outs) :]])

    return pl.pallas_call(
        body,
        grid_spec=pltpu.PrefetchScalarGridSpec(
            num_scalar_prefetch=1,
            grid=(1,),
            in_specs=[whole(piece) for piece in pieces]
            + [pl.BlockSpec(memory_space=pl.ANY) for _ in earlier],
            out_specs=[
                pl.BlockSpec((1,) + shape, lambda at, core: (layer, 0, 0)) for shape in shapes
            ],
        ),
        out_shape=outs,
        input_output_aliases={1 + len(pieces) + at: at for at in range(len(earlier))},
        name=name,
    )(core, *given)


def by_core(core, own_ref, other_ref, body):
    pl.when(core == 0)(lambda: body(own_ref, other_ref))
    pl.when(core == 1)(lambda: body(other_ref, own_ref))


def merge_hidden(core, refs, outs):
    def body(first, second):
        half_width = outs[0].shape[1] // CORES
        part = half_width // merge_hidden.shards
        for at in range(merge_hidden.shards):
            for side, ref in enumerate((first, second)):
                start = (at * CORES + side) * part
                outs[0][:, start : start + part] = ref[:, at * part : (at + 1) * part].astype(F32)

    by_core(core, *refs, body)


def merge_rows(core, refs, outs):
    def body(first, second):
        rows = first.shape[0]
        outs[0][:rows, :] = first[...].astype(F32)
        outs[0][rows:, :] = second[...].astype(F32)

    by_core(core, *refs, body)


def merge_heads(core, refs, outs):
    qk_own, qk_other, vp_own, vp_other = refs

    def heads(first, second, lanes, start, count):
        for at in range(count):
            pair = [ref[:, lanes + at * HEAD_DIM : lanes + (at + 1) * HEAD_DIM] for ref in (first, second)]
            at_out = start + at * CORES * HEAD_DIM
            outs[0][:, at_out : at_out + CORES * HEAD_DIM] = jnp.concatenate(pair, axis=1).astype(F32)

    width = outs[1].shape[1]
    count = width // HEAD_DIM // CORES
    by_core(core, qk_own, qk_other, lambda one, two: heads(one, two, 0, 0, 2 * count))
    by_core(core, vp_own, vp_other, lambda one, two: heads(one, two, 0, 2 * width, count))

    def rows(first, second):
        for side, ref in enumerate((first, second)):
            for part in range(2):
                outs[1][
                    side * HEAD_DIM : (side + 1) * HEAD_DIM,
                    part * (width // 2) : (part + 1) * (width // 2),
                ] = ref[part * HEAD_DIM : (part + 1) * HEAD_DIM, width // 2 :].astype(F32)

    by_core(core, vp_own, vp_other, rows)


def normed(stream, gain, offset):
    center = stream - jnp.mean(stream, axis=-1, keepdims=True)
    spread_of = jnp.mean(center * center, axis=-1, keepdims=True)
    return center * lax.rsqrt(spread_of + epsilon) * gain + offset


def norm_back(stream, gain, grad):
    center = stream - jnp.mean(stream, axis=-1, keepdims=True)
    spread_of = jnp.mean(center * center, axis=-1, keepdims=True)
    inverse = lax.rsqrt(spread_of + epsilon)
    hat = center * inverse
    scaled = grad * gain
    back = inverse * (
        scaled
        - jnp.mean(scaled, axis=-1, keepdims=True)
        - hat * jnp.mean(scaled * hat, axis=-1, keepdims=True)
    )
    return back, jnp.sum(grad * hat, axis=0), jnp.sum(grad, axis=0)


def exact_gelu(values):
    return jax.nn.gelu(values, approximate=False)


def dot(left, right, left_at, right_at):
    return lax.dot_general(
        left, right, (((left_at,), (right_at,)), ((), ())), preferred_element_type=F32
    )


def softmax_of(query, key, dead):
    scores = dot(query, key, 1, 1)
    scores = jnp.where(dead, masked_score, scores)
    raised = jnp.exp(scores - jnp.max(scores, axis=1, keepdims=True))
    return raised / jnp.sum(raised, axis=1, keepdims=True)


def attend_kernel(live_ref, query_ref, key_ref, value_ref, out_ref):
    dead = live_ref[...] == 0.0
    outs = []
    for at in range(query_ref.shape[1] // HEAD_DIM):
        lanes = slice(at * HEAD_DIM, (at + 1) * HEAD_DIM)
        probs = softmax_of(query_ref[:, lanes], key_ref[:, lanes], dead).astype(BF)
        outs.append(dot(probs, value_ref[:, lanes], 1, 0))
    out_ref[...] = jnp.concatenate(outs, axis=1).astype(out_ref.dtype)


def attend_back_kernel(
    live_ref, query_ref, key_ref, value_ref, grad_ref, query_out, key_out, value_out
):
    dead = live_ref[...] == 0.0
    outs = ([], [], [])
    for at in range(query_ref.shape[1] // HEAD_DIM):
        lanes = slice(at * HEAD_DIM, (at + 1) * HEAD_DIM)
        query, key, value = query_ref[:, lanes], key_ref[:, lanes], value_ref[:, lanes]
        grad = grad_ref[:, lanes]
        probs = softmax_of(query, key, dead)
        prob_grad = dot(grad, value, 1, 1)
        inner = jnp.sum(probs * prob_grad, axis=1, keepdims=True)
        score_grad = (probs * (prob_grad - inner)).astype(BF)
        outs[0].append(dot(score_grad, key, 1, 0).astype(BF).astype(F32) * HEAD_DIM**-0.5)
        outs[1].append(dot(score_grad, query, 0, 0))
        outs[2].append(dot(probs.astype(BF), grad, 0, 0))
    for ref, parts in zip((query_out, key_out, value_out), outs):
        ref[...] = jnp.concatenate(parts, axis=1).astype(ref.dtype)


def attention(live, qkv):
    rows, columns = qkv.shape
    lanes = 2 * HEAD_DIM
    steps = columns // 3 // lanes

    def third(which):
        return pl.BlockSpec((rows, lanes), lambda at: (0, at + which * steps))

    return pl.pallas_call(
        attend_kernel,
        grid=(steps,),
        in_specs=[pl.BlockSpec((1, rows), lambda at: (0, 0)), third(0), third(1), third(2)],
        out_specs=third(0),
        out_shape=jax.ShapeDtypeStruct((rows, columns // 3), BF),
        cost_estimate=pl.CostEstimate(
            flops=4 * rows * rows * columns // 3,
            bytes_accessed=rows * columns * 3,
            transcendentals=rows * rows * columns // 3 // HEAD_DIM,
        ),
        name="attend",
    )(live, qkv, qkv, qkv)


def attention_back(live, qkv, grad):
    rows, columns = qkv.shape
    lanes = 2 * HEAD_DIM
    steps = columns // 3 // lanes

    def third(which):
        return pl.BlockSpec((rows, lanes), lambda at: (0, at + which * steps))

    out = jax.ShapeDtypeStruct((rows, columns // 3), BF)
    return pl.pallas_call(
        attend_back_kernel,
        grid=(steps,),
        in_specs=[
            pl.BlockSpec((1, rows), lambda at: (0, 0)),
            third(0),
            third(1),
            third(2),
            third(0),
        ],
        out_specs=[third(0)] * 3,
        out_shape=[out] * 3,
        cost_estimate=pl.CostEstimate(
            flops=10 * rows * rows * columns // 3,
            bytes_accessed=rows * columns * 5,
            transcendentals=rows * rows * columns // 3 // HEAD_DIM,
        ),
        name="attend_back",
    )(live, qkv, qkv, qkv, grad)


def row_sum(values):
    return jnp.sum(values.astype(F32), axis=0)


def pair_rows(own):
    return jnp.concatenate([own, swap_cores(own)], axis=0)


def pair_total(terms):
    rows = terms.shape[0] // CORES
    return terms[:rows] + swap_cores(terms[rows:].astype(BF)).astype(F32)


def column_trips(images):
    size = lax.axis_size("seq")
    trips = []
    for turn in range(images):
        pairs = []
        for core in range(CORES):
            for seq in range(size):
                image = (turn + seq) % images
                to_core, to_seq = seq // images, core * images + image
                pairs.append((core * size + seq, to_core * size + to_seq))
        trips.append(pairs)
    return trips


def to_chip(values, trips):
    images = values.shape[0]
    seq = lax.axis_index("seq")
    parts = []
    for turn, pairs in enumerate(trips):
        part = lax.dynamic_index_in_dim(values, (turn + seq) % images, 0, keepdims=False)
        parts.append(lax.ppermute(part, ("core", "seq"), pairs))
    return jnp.concatenate(parts, axis=0)


def from_chip_steps(values, trips):
    images = len(trips)
    rows = values.shape[0] // images
    seq = lax.axis_index("seq")
    back = []
    for turn, pairs in enumerate(trips):
        part = values[turn * rows : (turn + 1) * rows]
        back.append((yield ("core", "seq"), [(there, here) for here, there in pairs], part))
    stacked = jnp.stack(back)
    return jnp.stack(
        [
            lax.dynamic_index_in_dim(stacked, (image - seq) % images, 0, keepdims=False)
            for image in range(images)
        ]
    ).astype(F32)


def half(values, axis):
    return lax.dynamic_index_in_dim(values, lax.axis_index("core"), axis, keepdims=False)


def on_device(
    image_tokens,
    cotangent,
    ln1_gain,
    ln1_bias,
    qkv_weight,
    qv_bias,
    proj_weight,
    proj_bias,
    ln2_gain,
    ln2_bias,
    fc1_weight,
    fc1_bias,
    fc2_weight,
    fc2_bias,
):
    layers, own_width = ln1_gain.shape
    width = proj_weight.shape[2]
    hidden_width = fc1_weight.shape[2]
    shards = width // own_width
    images, rows_here = image_tokens.shape[:2]
    seq_size = lax.axis_size("seq")
    assert images * CORES == seq_size
    core, seq = lax.axis_index("core"), lax.axis_index("seq")
    trips = column_trips(images)

    small = jnp.concatenate(
        [
            member.reshape(layers, -1, own_width)
            for member in (
                ln1_gain,
                ln1_bias,
                qv_bias,
                proj_bias,
                ln2_gain,
                ln2_bias,
                fc2_bias,
                fc1_bias,
            )
        ],
        axis=1,
    )
    small = gather_small(small)

    def vector(layer, at):
        return small[:, layer, at].reshape(-1).astype(F32)

    def half_vector(layer, at):
        return half(small[:, layer, at].reshape(shards, CORES, -1), 1).reshape(-1).astype(F32)

    def small_of(layer):
        return (
            vector(layer, 0),
            vector(layer, 1),
            half_vector(layer, 2),
            half_vector(layer, 3),
            vector(layer, 4),
            vector(layer, 5),
            vector(layer, 6),
            vector(layer, 7),
            half(small[:, layer, 8:].reshape(shards, CORES, -1), 1).reshape(-1).astype(F32),
        )

    def weight_pieces(layer):
        qkv = half(qkv_weight[layer].reshape(own_width, 3, -1, CORES, HEAD_DIM), 3)
        proj = half(proj_weight[layer].reshape(CORES, -1, width), 0)
        fc1 = half(
            fc1_weight[layer].reshape(own_width, shards, CORES, hidden_width // shards // CORES),
            2,
        )
        fc2 = half(fc2_weight[layer].reshape(CORES, -1, width), 0)
        qkv = qkv.reshape(own_width, -1)
        proj = jnp.concatenate([proj[:, : width // 2], proj[:, width // 2 :]], axis=0)
        return (
            qkv[:, :width],
            jnp.concatenate([qkv[:, width:], proj], axis=1),
            fc1.reshape(own_width, -1),
            fc2,
        )

    stream = to_chip(image_tokens, trips).astype(F32)
    grad_stream = to_chip(cotangent, trips).astype(F32)

    def positions(which):
        turns = [
            (which * images + (seq - turn) % images) * rows_here + jnp.arange(rows_here)
            for turn in range(images)
        ]
        return jnp.concatenate(turns)

    own_live = (positions(core) < SEQ).astype(F32)
    other_live = (positions(1 - core) < SEQ).astype(F32)
    live = jnp.concatenate([own_live, other_live])[None]
    grad_stream = grad_stream * own_live[:, None]

    score_scale = HEAD_DIM**-0.5
    assert layers == 2 and own_width == CORES * HEAD_DIM
    assert lax.axis_size("shard") == 2
    line = Line()
    weights = [weight_pieces(layer) for layer in range(layers)]
    small_mats = [small_of(layer) for layer in range(layers)]

    def attend_forward(layer, stream, qk_mat, vp_mat):
        gain_one, bias_one, q_add, v_add, proj_add, gain_two, bias_two, _, _ = small_mats[layer]
        first_in = pair_rows(normed(stream, gain_one, bias_one).astype(BF))
        part = q_add.shape[0]
        qk = dot(first_in, qk_mat, 1, 0)
        value = dot(first_in, vp_mat[:, :part], 1, 0)
        qkv = jnp.concatenate(
            [(qk[:, :part] + q_add) * score_scale, qk[:, part:], value + v_add], axis=1
        ).astype(BF)
        attn_out = attention(live, qkv)
        proj_mat = vp_mat[:, part:].reshape(shards, 2, HEAD_DIM, width // 2)
        proj_mat = jnp.moveaxis(proj_mat, 1, 2).reshape(part, width)
        middle = stream + pair_total(dot(attn_out, proj_mat, 1, 0)) + proj_add
        second_in = pair_rows(normed(middle, gain_two, bias_two).astype(BF))
        return first_in, qkv, attn_out, middle, second_in, proj_mat

    def hidden_forward(layer, second_in, hid_mat):
        pre_act = dot(second_in, hid_mat, 1, 0) + small_mats[layer][8]
        return pre_act, exact_gelu(pre_act).astype(BF)

    def out_forward(layer, middle, hidden, out_mat):
        return middle + pair_total(dot(hidden, out_mat, 1, 0)) + small_mats[layer][7]

    def out_backward(branch, pre_act, out_mat):
        hidden_grad = dot(branch, out_mat, 1, 1)
        return jax.vjp(exact_gelu, pre_act)[1](hidden_grad)[0].astype(BF)

    def hidden_backward(layer, grad_stream, pre_grad, second_in, middle, hid_mat):
        hid_terms = dot(second_in, pre_grad, 0, 0).astype(BF)
        second_grad = pair_total(dot(pre_grad, hid_mat, 1, 1))
        back, grad_gain, grad_bias = norm_back(middle, small_mats[layer][5], second_grad)
        middle_grad = grad_stream + back
        proj_own = middle_grad.astype(BF)
        return hid_terms, middle_grad, proj_own, pair_rows(proj_own), grad_gain, grad_bias

    def attend_backward(layer, middle_grad, proj_grad, saved, mats):
        stream, first_in, qkv, attn_out, proj_mat = saved
        qk_mat, vp_mat = mats
        part = attn_out.shape[1]
        attn_grad = dot(proj_grad, proj_mat, 1, 1).astype(BF)
        query_grad, key_grad, value_grad = attention_back(live, qkv, attn_grad)
        qk_grad = jnp.concatenate([query_grad, key_grad], axis=1)
        qk_terms = dot(first_in, qk_grad, 0, 0).astype(BF)
        v_terms = dot(first_in, value_grad, 0, 0).astype(BF)
        proj_terms = dot(attn_out, proj_grad, 0, 0).astype(BF)
        proj_terms = proj_terms.reshape(shards, HEAD_DIM, 2, width // 2)
        proj_terms = jnp.moveaxis(proj_terms, 1, 2).reshape(width, part)
        vp_terms = jnp.concatenate([v_terms, proj_terms], axis=1)
        first_grad = pair_total(
            dot(qk_grad, qk_mat, 1, 1) + dot(value_grad, vp_mat[:, :part], 1, 1)
        )
        back, grad_gain, grad_bias = norm_back(stream, small_mats[layer][0], first_grad)
        return (
            qk_terms,
            vp_terms,
            middle_grad + back,
            query_grad,
            value_grad,
            grad_gain,
            grad_bias,
        )

    tasks = [[None] * 4 for _ in range(layers)]

    def gather(layer, at):
        tasks[layer][at] = line.add(gather_steps(weights[layer][at]))

    def mat(layer, at):
        return tasks[layer][at].value

    gather(0, 0)
    line.tick()
    gather(0, 1)
    line.tick()
    gather(0, 2)
    line.tick()
    gather(0, 3)
    line.tick()
    gather(1, 0)
    gather(1, 1)
    line.tick()
    gather(1, 2)
    (stream,) = line.tick(stream)
    streams = [stream]
    first = [attend_forward(0, stream, mat(0, 0), mat(0, 1))]
    gather(1, 3)
    *head, second_in, proj_mat = line.tick(*first[0])
    first[0] = (*head, second_in, proj_mat)
    hid = [hidden_forward(0, second_in, mat(0, 2))]
    hid[0] = line.tick(*hid[0])
    stream = out_forward(0, first[0][3], hid[0][1], mat(0, 3))
    branch_own = grad_stream.astype(BF)
    branch = pair_rows(branch_own)
    stream, branch = line.tick(stream, branch)
    streams.append(stream)
    first.append(attend_forward(1, stream, mat(1, 0), mat(1, 1)))
    first[1] = line.tick(*first[1])
    hid.append(hidden_forward(1, first[1][4], mat(1, 2)))
    out_terms = dot(hid[1][1], branch, 0, 0).astype(BF)
    *hid[1], out_terms = line.tick(*hid[1], out_terms)

    merged = [None] * 3
    owned = [[None] * 4 for _ in range(layers)]

    def reduce(layer, at, terms):
        owned[layer][at] = line.add(reduce_steps(terms))

    small_terms = [None] * layers
    output_task = None
    for layer in reversed(range(layers)):
        first_in, qkv, attn_out, middle, second_in, proj_mat = first[layer]
        pre_act, hidden = hid[layer]
        if layer < layers - 1:
            branch_own = grad_stream.astype(BF)
            branch = pair_rows(branch_own)
            out_terms = dot(hidden, branch, 0, 0).astype(BF)
        else:
            stream = out_forward(layer, middle, hidden, mat(layer, 3))
        if layer == layers - 1:
            reduce(layer, 3, out_terms)
            (branch,) = line.tick(branch)
            pre_grad = out_backward(branch, pre_act, mat(layer, 3))
            output_task = line.add(from_chip_steps(stream.astype(BF), trips))
        else:
            pre_grad = out_backward(branch, pre_act, mat(layer, 3))
            reduce(layer, 3, out_terms)
        (pre_grad,) = line.tick(pre_grad)
        hid_terms, middle_grad, proj_own, proj_grad, grad_gain_two, grad_bias_two = (
            hidden_backward(layer, grad_stream, pre_grad, second_in, middle, mat(layer, 2))
        )
        reduce(layer, 2, hid_terms)
        proj_grad, middle_grad = line.tick(proj_grad, middle_grad)
        (
            qk_terms,
            vp_terms,
            grad_next,
            query_grad,
            value_grad,
            grad_gain_one,
            grad_bias_one,
        ) = attend_backward(
            layer,
            middle_grad,
            proj_grad,
            (streams[layer], first_in, qkv, attn_out, proj_mat),
            (mat(layer, 0), mat(layer, 1)),
        )

        def by_half(vector_half):
            mine = vector_half.reshape(shards, -1)
            none = jnp.zeros_like(mine)
            pair = [jnp.where(core == at, mine, none) for at in range(CORES)]
            return jnp.stack(pair, axis=1).reshape(shards, -1, own_width)

        def by_owner(vector_whole):
            return vector_whole.reshape(shards, 1, own_width)

        small_terms[layer] = jnp.concatenate(
            [
                by_owner(grad_gain_one),
                by_owner(grad_bias_one),
                by_half(row_sum(query_grad)),
                by_half(row_sum(value_grad)),
                by_owner(row_sum(proj_own)),
                by_owner(grad_gain_two),
                by_owner(grad_bias_two),
                by_owner(row_sum(branch_own)),
                by_half(row_sum(pre_grad)),
            ],
            axis=1,
        )
        reduce(layer, 0, qk_terms)
        reduce(layer, 1, vp_terms)
        grad_stream = grad_next
        if layer:
            grad_stream, small_terms[layer] = line.tick(grad_stream, small_terms[layer])
    terms = jnp.stack(small_terms, axis=1)
    terms = terms.reshape((lax.axis_size("shard"), seq_size) + terms.shape[1:])
    small_task = line.add(small_steps(terms))
    input_task = line.add(from_chip_steps(grad_stream.astype(BF), trips))
    while line.tasks:
        line.tick()
    owned_small = small_task.value

    merge_hidden.shards = shards
    big = [None] * 4
    for layer in reversed(range(layers)):
        pairs = [task.value for task in owned[layer]]
        earlier = lambda *which: [] if layer == layers - 1 else [big[at] for at in which]
        (big[3],) = merged_call(
            merge_rows, pairs[3], [(fc2_weight.shape[1], width)], layers, layer, earlier(3), "merge_rows"
        )
        (big[2],) = merged_call(
            merge_hidden, pairs[2], [(own_width, hidden_width)], layers, layer, earlier(2), "merge_hidden"
        )
        big[0], big[1] = merged_call(
            merge_heads,
            pairs[0] + pairs[1],
            [(own_width, 3 * width), (own_width, width)],
            layers,
            layer,
            earlier(0, 1),
            "merge_heads",
        )

    def member(at, count=1):
        return owned_small[:, at : at + count].reshape(layers, -1)

    return (
        output_task.value,
        input_task.value,
        member(0),
        member(1),
        big[0],
        owned_small[:, 2:4],
        big[1],
        member(4),
        member(5),
        member(6),
        big[2],
        member(8, fc1_bias.shape[1] // own_width),
        big[3],
        member(7),
    )


def solution(mesh):
    dp, shard, seq = (mesh.shape[name] for name in ("dp", "shard", "seq"))
    cores = Mesh(
        mesh.devices.reshape(dp // CORES, CORES, shard, seq), ("rep", "core", "shard", "seq")
    )
    images = P(("rep", "core", "shard"), "seq", None)
    vectors = P(None, ("shard", "seq"))
    matrices = P(None, ("shard", "seq"), None)
    pairs = P(None, None, ("shard", "seq"))
    params = (
        vectors,
        vectors,
        matrices,
        pairs,
        matrices,
        vectors,
        vectors,
        vectors,
        matrices,
        vectors,
        matrices,
        vectors,
    )
    return jax.shard_map(
        on_device,
        mesh=cores,
        in_specs=(images, images) + params,
        out_specs=(images, images) + params,
        check_vma=False,
    )
```
